32 devices in a mesh: slab: 4 (over y, x), cross: 8 (over z, core).
Axes of the slice: x: 2, y: 2, z: 4, core: 2. Of those that a mesh axis runs over, the one named last changes fastest.
Arguments:
- rhs: bfloat16 [4, 8, 32, 128, 128], P('slab', 'cross'), may hold values from -6 to 6
- m_blocks: bfloat16 [4, 8, 56, 3, 128, 128], P('slab', 'cross'), may hold values from -0.3125 to 0.3125
- m_cols: int32 [4, 8, 56, 3], P('slab', 'cross'), may hold values from 0 to 55, as said below
- j_blocks: bfloat16 [4, 8, 32, 3, 128, 128], P('slab', 'cross'), may hold values from -0.3125 to 0.3125
- j_cols: int32 [4, 8, 32, 3], P('slab', 'cross'), may hold values from 0 to 55, as said below
- send_list: int32 [4, 8, 8, 2], P('slab', 'cross'), may hold values from 0 to 31, as said below
- send_count: int32 [4, 8, 8], P('slab', 'cross'), may hold values from 0 to 2, as said below
Outputs:
- second_iterate: bfloat16 [4, 8, 32, 128, 128], P('slab', 'cross')
The draws below stay inside these ranges and needn't reach their ends.
Inputs may be any that keep to these rules, and one draw needn't show every extreme that they name: `m_cols`: each row's first block column is the row itself; the others differ from it and from each other. `j_cols`: each row's first block column is the row itself; the others differ from it and from each other. `send_list`: the used slots of one list name different block rows. `send_count`: no subdomain lends rows to itself; in every slab index some subdomain receives 2 rows from each other one.
All inputs are finite; a program needn't handle non-finite values.
Results may differ from the reference program's by a relative error of at most 0.0058.
Values may be sent and summed in bfloat16 or wider, within the bound.
A program may use at most 64 MiB of HBM per device.

```python
import jax
import jax.numpy as jnp
from jax import lax

BLK = 128
NV = 128
ROWS = 32
OVL = 4
CAP = 2
NBLK = 3
EXT = 56
N_SLAB = 4
N_CROSS = 8


def pattern_cols(key, row_total, span):
    leading = (N_SLAB, N_CROSS, row_total)
    row_ids = jnp.arange(row_total, dtype=jnp.int32)
    columns = [jnp.broadcast_to(row_ids, leading)]
    for slot_num in range(1, NBLK):
        lower_end = 1 + (slot_num - 1) * (span - 1) // (NBLK - 1)
        upper_end = 1 + slot_num * (span - 1) // (NBLK - 1)
        offset = jax.random.randint(jax.random.fold_in(key, slot_num), leading, lower_end, upper_end, dtype=jnp.int32)
        columns.append((row_ids + offset) % span)
    return jnp.stack(columns, axis=-1)


def draw_m_cols(key, part):
    return pattern_cols(jax.random.fold_in(key, 11), EXT, EXT)


def draw_j_cols(key, part):
    columns = pattern_cols(jax.random.fold_in(key, 23), ROWS, EXT)
    return columns.at[0, 0, 0, NBLK - 1].set(EXT - 1)


def draw_send_count(key, part):
    counts = jax.random.randint(jax.random.fold_in(key, 31), (N_SLAB, N_CROSS, N_CROSS), 0, CAP + 1, dtype=jnp.int32)
    chosen = jax.random.randint(jax.random.fold_in(key, 37), (N_SLAB,), 0, N_CROSS, dtype=jnp.int32)
    peer_ids = jnp.arange(N_CROSS, dtype=jnp.int32)
    filled = peer_ids[None, None, :] == chosen[:, None, None]
    counts = jnp.where(filled, CAP, counts)
    itself = peer_ids[None, :, None] == peer_ids[None, None, :]
    return jnp.where(itself, 0, counts).astype(jnp.int32)


def draw_send_list(key, part):
    starts = jax.random.randint(jax.random.fold_in(key, 41), (N_SLAB, N_CROSS, N_CROSS), 0, ROWS, dtype=jnp.int32)
    starts = starts.at[0, 0, 0].set(ROWS - 1).at[0, 0, 1].set(0)
    slots = [starts]
    for slot_num in range(1, CAP):
        lower_end = slot_num * ROWS // CAP
        upper_end = (slot_num + 1) * ROWS // CAP
        offset = jax.random.randint(jax.random.fold_in(key, 50 + slot_num), (N_SLAB, N_CROSS, N_CROSS), lower_end, upper_end, dtype=jnp.int32)
        slots.append((starts + offset) % ROWS)
    return jnp.stack(slots, axis=-1).astype(jnp.int32)


def level_of(key, dims, shards, low, top_value):
    level, own = 1.0, jax.random.fold_in(key, 6)
    for position, parts in shards:
        steps = jnp.exp(jax.random.uniform(jax.random.fold_in(own, position), (parts,), jnp.float32, low / len(shards), top_value / len(shards)))
        level = level * jnp.repeat(steps, dims[position] // parts).reshape([-1 if axis == position else 1 for axis in range(len(dims))])
    return level


def noise(rng, shape, scale, limit, split=(), kind=jnp.bfloat16):
    loudness = level_of(rng, shape, split, -0.22, 0.18) if split else 1.0
    values = jax.random.normal(rng, shape, jnp.float32) * scale * loudness
    return jnp.minimum(jnp.maximum(values, -limit), limit).astype(kind)


def setup_inputs(seed: int = 0) -> dict:
    streams_of = jax.random.split(jax.random.key(seed), 8)
    return {
        "rhs": noise(streams_of[0], (N_SLAB, N_CROSS, ROWS, BLK, NV), 1.0, 6.0, ((0, 4), (1, 8))),
        "m_blocks": noise(streams_of[1], (N_SLAB, N_CROSS, EXT, NBLK, BLK, BLK), (NBLK * BLK) ** -0.5, 0.3125, ((0, 4), (1, 8))),
        "m_cols": draw_m_cols(jax.random.fold_in(streams_of[7], 71), 0),
        "j_blocks": noise(streams_of[3], (N_SLAB, N_CROSS, ROWS, NBLK, BLK, BLK), (NBLK * BLK) ** -0.5, 0.3125, ((0, 4), (1, 8))),
        "j_cols": draw_j_cols(jax.random.fold_in(streams_of[7], 71), 0),
        "send_list": draw_send_list(jax.random.fold_in(streams_of[7], 71), 0),
        "send_count": draw_send_count(jax.random.fold_in(streams_of[7], 71), 0),
    }


def extend_all(field, send_list, send_count):
    zeros = jnp.zeros_like(field[:1, :, :OVL])
    upper = jnp.concatenate([zeros, field[:-1, :, ROWS - OVL:]], axis=0)
    lower = jnp.concatenate([field[1:, :, :OVL], zeros], axis=0)
    picked = jax.vmap(jax.vmap(lambda source_rows, picks: jnp.take(source_rows, picks.reshape(-1), axis=0)))(field, send_list)
    picked = picked.reshape(N_SLAB, N_CROSS, N_CROSS, CAP, BLK, NV)
    valid = jnp.arange(CAP, dtype=jnp.int32)[None, None, None, :] < send_count[..., None]
    picked = jnp.where(valid[..., None, None], picked, jnp.zeros((), field.dtype))
    arrived = jnp.swapaxes(picked, 1, 2).reshape(N_SLAB, N_CROSS, N_CROSS * CAP, BLK, NV)
    return jnp.concatenate([field, upper, lower, arrived], axis=2)


def apply_blocks(blocks, columns, extended):
    flat_blocks = blocks.reshape((N_SLAB * N_CROSS,) + blocks.shape[2:])
    flat_cols = columns.reshape((N_SLAB * N_CROSS,) + columns.shape[2:])
    flat_ext = extended.reshape((N_SLAB * N_CROSS,) + extended.shape[2:])

    def single(items):
        block_set, col_set, ext_set = items
        gathered = jnp.take(ext_set, col_set, axis=0).astype(jnp.float32)
        return jnp.einsum('ekab,ekbn->ean', block_set.astype(jnp.float32), gathered)

    result = lax.map(single, (flat_blocks, flat_cols, flat_ext))
    return result.reshape((N_SLAB, N_CROSS) + result.shape[1:])


def assemble(partial_value, send_list, send_count):
    total = partial_value[:, :, :ROWS].astype(jnp.float32)
    upper_part = partial_value[:, :, ROWS:ROWS + OVL]
    lower_part = partial_value[:, :, ROWS + OVL:ROWS + 2 * OVL]
    zeros = jnp.zeros_like(upper_part[:1])
    from_prev = jnp.concatenate([zeros, lower_part[:-1]], axis=0).astype(jnp.float32)
    from_next = jnp.concatenate([upper_part[1:], zeros], axis=0).astype(jnp.float32)
    total = total.at[:, :, :OVL].add(from_prev)
    total = total.at[:, :, ROWS - OVL:].add(from_next)
    cross_part = partial_value[:, :, ROWS + 2 * OVL:].reshape(N_SLAB, N_CROSS, N_CROSS, CAP, BLK * NV)
    returned = jnp.swapaxes(cross_part, 1, 2).reshape(N_SLAB, N_CROSS, N_CROSS * CAP, BLK * NV).astype(jnp.float32)
    valid = (jnp.arange(CAP, dtype=jnp.int32)[None, None, None, :] < send_count[..., None]).reshape(N_SLAB, N_CROSS, N_CROSS * CAP)
    targets = send_list.reshape(N_SLAB, N_CROSS, N_CROSS * CAP)
    table = ((targets[:, :, None, :] == jnp.arange(ROWS, dtype=jnp.int32)[None, None, :, None]) & valid[:, :, None, :]).astype(jnp.float32)
    added = jnp.einsum('scrj,scjm->scrm', table, returned, precision=lax.Precision.HIGHEST)
    return total + added.reshape(N_SLAB, N_CROSS, ROWS, BLK, NV)


def precondition(field, m_blocks, m_cols, send_list, send_count):
    extended = extend_all(field, send_list, send_count)
    partial_value = apply_blocks(m_blocks, m_cols, extended).astype(jnp.bfloat16)
    return assemble(partial_value, send_list, send_count)


def reference(rhs, m_blocks, m_cols, j_blocks, j_cols, send_list, send_count):
    first = precondition(rhs, m_blocks, m_cols, send_list, send_count).astype(jnp.bfloat16)
    extended = extend_all(first, send_list, send_count)
    image = apply_blocks(j_blocks, j_cols, extended)
    residual = (rhs.astype(jnp.float32) - image).astype(jnp.bfloat16)
    second = first.astype(jnp.float32) + precondition(residual, m_blocks, m_cols, send_list, send_count)
    return second.astype(jnp.bfloat16)
```

```python
import functools

import jax
import jax.numpy as jnp
from jax import lax
from jax.experimental import pallas as pl
from jax.experimental.pallas import tpu as pltpu
from jax.sharding import PartitionSpec as P

MESH = pl.DeviceIdType.MESH
F32 = jnp.float32
BF16 = jnp.bfloat16


def kernel(
    n_slab, n, ovl,
    rhs_hbm, m_hbm, j_hbm, m_cols, j_cols, targets, counts,
    out_ref,
    m_v, j_v, own0, own1, own2, ext0, ext1, ext2, part, send_buf, ret, ret_slab, run, acc,
    prev, last, load_sem, send_sem, recv_sem,
):
    s = lax.axis_index("slab")
    c = lax.axis_index("cross")
    own = (own0, own1, own2)
    ext = (ext0, ext1, ext2)
    rows = own0.shape[0]
    cap = send_buf.shape[2]
    kcount = m_v.shape[1]
    base = rows + 2 * ovl
    slots = (n - 1) * cap
    zero_slot = slots
    up_i, down_i = n, n + 1
    has_up = s > 0
    has_down = s < n_slab - 1

    def peer(d):
        return lax.rem(c + d, n)

    def order(t):
        return n // 2 + (1 - 2 * lax.rem(t, 2)) * ((t + 1) // 2)

    load_own = pltpu.make_async_copy(rhs_hbm.at[0, 0], own0, load_sem.at[0])
    load_ext = pltpu.make_async_copy(rhs_hbm.at[0, 0], ext0.at[pl.ds(0, rows)], load_sem.at[1])
    load_m = pltpu.make_async_copy(m_hbm.at[0, 0], m_v, load_sem.at[2])
    load_j = pltpu.make_async_copy(j_hbm.at[0, 0], j_v, load_sem.at[3])
    load_own.start()
    load_ext.start()
    load_m.start()
    load_j.start()

    barrier = pltpu.get_barrier_semaphore()

    @pl.loop(1, n)
    def _(d):
        pl.semaphore_signal(barrier, inc=1, device_id=(s, peer(d)), device_id_type=MESH)

    @pl.when(has_up)
    def _():
        pl.semaphore_signal(barrier, inc=1, device_id=(s - 1, c), device_id_type=MESH)

    @pl.when(has_down)
    def _():
        pl.semaphore_signal(barrier, inc=1, device_id=(s + 1, c), device_id_type=MESH)

    zero_tile = jnp.zeros(own0.shape[1:], BF16)
    for r in range(3):
        for t in range(cap):
            ext[r][base + c * cap + t] = zero_tile

    @pl.when(jnp.logical_not(has_up))
    def _():
        for r in range(3):
            for t in range(ovl):
                ext[r][rows + t] = zero_tile
        for r in range(2):
            for t in range(ovl):
                ret_slab[r, t] = zero_tile

    @pl.when(jnp.logical_not(has_down))
    def _():
        for r in range(3):
            for t in range(ovl):
                ext[r][rows + ovl + t] = zero_tile
        for r in range(2):
            for t in range(ovl):
                ret_slab[r, ovl + t] = zero_tile

    run[zero_slot] = jnp.zeros(own0.shape[1:], F32)

    def slab_copy(src, dst, r, mine, theirs, to):
        return pltpu.make_async_remote_copy(
            src_ref=src, dst_ref=dst, send_sem=send_sem.at[r, mine], recv_sem=recv_sem.at[r, theirs],
            device_id=(to, c), device_id_type=MESH,
        )

    def lend_up(e, r):
        return slab_copy(ext[e].at[pl.ds(0, ovl)], ext[e].at[pl.ds(rows + ovl, ovl)], r, up_i, down_i, s - 1)

    def lend_down(e, r):
        return slab_copy(ext[e].at[pl.ds(rows - ovl, ovl)], ext[e].at[pl.ds(rows, ovl)], r, down_i, up_i, s + 1)

    def lend_cross(e, r, d):
        return pltpu.make_async_remote_copy(
            src_ref=send_buf.at[e, d - 1], dst_ref=ext[e].at[pl.ds(base + c * cap, cap)],
            send_sem=send_sem.at[r, d], recv_sem=recv_sem.at[r, n - d],
            device_id=(s, peer(d)), device_id_type=MESH,
        )

    def got_cross(e, r, d):
        return pltpu.make_async_remote_copy(
            src_ref=send_buf.at[e, d - 1], dst_ref=ext[e].at[pl.ds(base + peer(d) * cap, cap)],
            send_sem=send_sem.at[r, d], recv_sem=recv_sem.at[r, d],
            device_id=(s, peer(d)), device_id_type=MESH,
        )

    def got_up(e, r):
        return slab_copy(ext[e].at[pl.ds(0, ovl)], ext[e].at[pl.ds(rows, ovl)], r, up_i, up_i, s - 1)

    def got_down(e, r):
        return slab_copy(ext[e].at[pl.ds(0, ovl)], ext[e].at[pl.ds(rows + ovl, ovl)], r, down_i, down_i, s + 1)

    def lend_slab(e, r):
        @pl.when(has_up)
        def _():
            lend_up(e, r).start()

        @pl.when(has_down)
        def _():
            lend_down(e, r).start()

    def lend_rows(e, r):
        @pl.loop(0, n - 1)
        def _(step):
            d = order(step)
            q = peer(d)
            for t in range(cap):
                picked = own[e][targets[0, 0, t, q]]
                used = t < counts[0, 0, q]
                send_buf[e, d - 1, t] = jnp.where(used, picked, jnp.zeros_like(picked))
            lend_cross(e, r, d).start()

    def await_lent(e, r):
        @pl.when(has_up)
        def _():
            got_up(e, r).wait_recv()

        @pl.when(has_down)
        def _():
            got_down(e, r).wait_recv()

        @pl.loop(1, n)
        def _(d):
            got_cross(e, r, d).wait_recv()

    def finish_lend(e, r):
        @pl.when(has_up)
        def _():
            lend_up(e, r).wait_send()

        @pl.when(has_down)
        def _():
            lend_down(e, r).wait_send()

        @pl.loop(1, n)
        def _(d):
            lend_cross(e, r, d).wait_send()

    def back_up(a, r):
        return slab_copy(part.at[a, pl.ds(rows, ovl)], ret_slab.at[a, pl.ds(ovl, ovl)], r, up_i, down_i, s - 1)

    def back_down(a, r):
        return slab_copy(part.at[a, pl.ds(rows + ovl, ovl)], ret_slab.at[a, pl.ds(0, ovl)], r, down_i, up_i, s + 1)

    def home_up(a, r):
        return slab_copy(part.at[a, pl.ds(rows, ovl)], ret_slab.at[a, pl.ds(0, ovl)], r, up_i, up_i, s - 1)

    def home_down(a, r):
        return slab_copy(part.at[a, pl.ds(rows, ovl)], ret_slab.at[a, pl.ds(ovl, ovl)], r, down_i, down_i, s + 1)

    def back_cross(a, r, d):
        return pltpu.make_async_remote_copy(
            src_ref=part.at[a, pl.ds(base + peer(d) * cap, cap)], dst_ref=ret.at[a, n - d - 1],
            send_sem=send_sem.at[r, d], recv_sem=recv_sem.at[r, n - d],
            device_id=(s, peer(d)), device_id_type=MESH,
        )

    def home_cross(a, r, d):
        return pltpu.make_async_remote_copy(
            src_ref=part.at[a, pl.ds(base + peer(d) * cap, cap)], dst_ref=ret.at[a, d - 1],
            send_sem=send_sem.at[r, d], recv_sem=recv_sem.at[r, d],
            device_id=(s, peer(d)), device_id_type=MESH,
        )

    def row_product(blocks, cols, e, i, k0=0):
        left = jnp.concatenate([blocks[i, k] for k in range(k0, kcount)], axis=1)
        right = jnp.concatenate([ext[e][cols[0, k, 0, i]] for k in range(k0, kcount)], axis=0)
        return jnp.dot(left, right, preferred_element_type=F32)

    def partial_row(a, e, i):
        part[a, i] = row_product(m_v, m_cols, e, i).astype(BF16)

    def apply_and_return(a, e, r):
        @pl.loop(0, n - 1)
        def _(step):
            d = order(step)
            first_row = base + peer(d) * cap
            for t in range(cap):
                partial_row(a, e, first_row + t)
            back_cross(a, r, d).start()

        @pl.loop(0, 2 * ovl // 4)
        def _(g):
            for t in range(4):
                partial_row(a, e, rows + 4 * g + t)

        @pl.when(has_up)
        def _():
            back_up(a, r).start()

        @pl.when(has_down)
        def _():
            back_down(a, r).start()

        @pl.loop(0, rows // 4)
        def _(g):
            for t in range(4):
                partial_row(a, e, 4 * g + t)

    def await_returns(a, r):
        @pl.loop(1, n)
        def _(d):
            home_cross(a, r, d).wait_recv()
            for t in range(cap):
                p = (d - 1) * cap + t
                run[p] = ret[a, d - 1, t].astype(F32) + run[prev[p]]

        @pl.when(has_up)
        def _():
            home_up(a, r).wait_recv()

        @pl.when(has_down)
        def _():
            home_down(a, r).wait_recv()

    def finish_return(a, r):
        @pl.when(has_up)
        def _():
            back_up(a, r).wait_send()

        @pl.when(has_down)
        def _():
            back_down(a, r).wait_send()

        @pl.loop(1, n)
        def _(d):
            back_cross(a, r, d).wait_send()

    def assembled(a, body):
        def total(i):
            return part[a, i].astype(F32) + run[last[i]]

        @pl.loop(0, ovl)
        def _(i):
            body(i, total(i) + ret_slab[a, i].astype(F32))

        @pl.loop(0, ovl)
        def _(t):
            i = rows - ovl + t
            body(i, total(i) + ret_slab[a, ovl + t].astype(F32))

        @pl.loop(ovl, rows - ovl)
        def _(i):
            body(i, total(i))

    load_own.wait()
    load_ext.wait()

    pl.semaphore_wait(barrier, n - 1 + has_up.astype(jnp.int32) + has_down.astype(jnp.int32))

    lend_slab(0, 0)
    lend_rows(0, 0)

    def key_of(p):
        q = peer(p // cap + 1)
        t = lax.rem(p, cap)
        return jnp.where(t < counts[0, 0, q], targets[0, 0, t, q], -1)

    @pl.loop(0, rows)
    def _(i):
        last[i] = zero_slot

    keys = [key_of(p) for p in range(slots)]
    for p in range(slots):
        found = zero_slot
        for p2 in range(p):
            found = jnp.where(keys[p2] == keys[p], p2, found)
        prev[p] = jnp.where(keys[p] < 0, zero_slot, found)

    @pl.loop(0, rows)
    def _(i):
        found = zero_slot
        for p in range(slots):
            found = jnp.where(keys[p] == i, p, found)
        last[i] = found

    load_m.wait()
    load_j.wait()
    await_lent(0, 0)

    apply_and_return(0, 0, 1)
    await_returns(0, 1)

    def put_first(i, value):
        rounded = value.astype(BF16)
        own[1][i] = rounded
        ext[1][i] = rounded

    assembled(0, put_first)

    lend_slab(1, 2)
    lend_rows(1, 2)

    @pl.loop(0, rows // 4)
    def _(g):
        for t in range(4):
            i = 4 * g + t
            acc[i] = own[0][i].astype(F32) - jnp.dot(j_v[i, 0], own[1][i], preferred_element_type=F32)

    await_lent(1, 2)

    @pl.loop(0, rows // 4)
    def _(g):
        for t in range(4):
            i = 4 * g + t
            rounded = (acc[i] - row_product(j_v, j_cols, 1, i, 1)).astype(BF16)
            own[2][i] = rounded
            ext[2][i] = rounded

    lend_slab(2, 3)
    lend_rows(2, 3)
    await_lent(2, 3)

    apply_and_return(1, 2, 4)
    await_returns(1, 4)

    def put_second(i, value):
        out_ref[0, 0, i] = (own[1][i].astype(F32) + value).astype(BF16)

    assembled(1, put_second)

    finish_lend(0, 0)
    finish_return(0, 1)
    finish_lend(1, 2)
    finish_lend(2, 3)
    finish_return(1, 4)


def solution(mesh):
    n_slab = mesh.shape["slab"]
    n = mesh.shape["cross"]

    def per_device(rhs, m_blocks, m_cols, j_blocks, j_cols, send_list, send_count):
        rows, blk, nv = rhs.shape[2:]
        total_rows, kcount = m_blocks.shape[2:4]
        cap = send_list.shape[3]
        ovl = (total_rows - rows - n * cap) // 2
        slots = (n - 1) * cap
        tile = (blk, nv)
        smem = pl.BlockSpec(memory_space=pltpu.SMEM)
        hbm = pl.BlockSpec(memory_space=pl.ANY)
        return pl.pallas_call(
            functools.partial(kernel, n_slab, n, ovl),
            out_shape=jax.ShapeDtypeStruct(rhs.shape, rhs.dtype),
            in_specs=[hbm, hbm, hbm, smem, smem, smem, smem],
            out_specs=pl.BlockSpec(memory_space=pltpu.VMEM),
            scratch_shapes=[
                pltpu.VMEM(m_blocks.shape[2:], BF16),
                pltpu.VMEM(j_blocks.shape[2:], BF16),
                *([pltpu.VMEM((rows,) + tile, BF16)] * 3),
                *([pltpu.VMEM((total_rows,) + tile, BF16)] * 3),
                pltpu.VMEM((2, total_rows) + tile, BF16),
                pltpu.VMEM((3, n - 1, cap) + tile, BF16),
                pltpu.VMEM((2, n - 1, cap) + tile, BF16),
                pltpu.VMEM((2, 2 * ovl) + tile, BF16),
                pltpu.VMEM((slots + 1,) + tile, F32),
                pltpu.VMEM((rows,) + tile, F32),
                pltpu.SMEM((slots,), jnp.int32),
                pltpu.SMEM((rows,), jnp.int32),
                pltpu.SemaphoreType.DMA((4,)),
                pltpu.SemaphoreType.DMA((5, n + 2)),
                pltpu.SemaphoreType.DMA((5, n + 2)),
            ],
            compiler_params=pltpu.CompilerParams(
                collective_id=0, has_side_effects=True, vmem_limit_bytes=60 * 1024 * 1024
            ),
        )(
            rhs, m_blocks, j_blocks, m_cols.transpose(0, 3, 1, 2), j_cols.transpose(0, 3, 1, 2),
            send_list.transpose(0, 1, 3, 2), send_count,
        )

    return jax.shard_map(
        per_device,
        mesh=mesh,
        in_specs=(
            P("slab", "cross", None, None, None),
            P("slab", "cross", None, None, None, None),
            P("slab", "cross", None, None),
            P("slab", "cross", None, None, None, None),
            P("slab", "cross", None, None),
            P("slab", "cross", None, None),
            P("slab", "cross", None),
        ),
        out_specs=P("slab", "cross", None, None, None),
        check_vma=False,
    )
```

```python
import functools

import jax
import jax.numpy as jnp
from jax import lax
from jax.experimental import pallas as pl
from jax.experimental.pallas import tpu as pltpu
from jax.sharding import PartitionSpec as P

MESH = pl.DeviceIdType.MESH
F32 = jnp.float32
BF16 = jnp.bfloat16


def kernel(
    n_slab, n, ovl,
    rhs_hbm, m_hbm, j_hbm, m_cols, j_cols, targets, counts,
    out_ref,
    m_v, j_v, raw, own1a, own1b, own2a, own2b, ext0a, ext0b, ext1a, ext1b, ext2a, ext2b, part, send_buf, ret, ret_slab, run, acc,
    prev, last, load_sem, send_sem, recv_sem,
):
    s = lax.axis_index("slab")
    c = lax.axis_index("cross")
    own = ((raw, raw), (own1a, own1b), (own2a, own2b))
    ext = ((ext0a, ext0b), (ext1a, ext1b), (ext2a, ext2b))
    rows = raw.shape[0]
    halves = (0, 1)
    width = ext0a.shape[1]
    tile = ext0a.shape[1:]
    cap = send_buf.shape[3]
    kcount = m_v.shape[1]
    base = rows + 2 * ovl
    slots = (n - 1) * cap
    zero_slot = slots
    up_i, down_i = n, n + 1
    has_up = s > 0
    has_down = s < n_slab - 1

    def peer(d):
        return lax.rem(c + d, n)

    def order(t):
        return n // 2 + (1 - 2 * lax.rem(t, 2)) * ((t + 1) // 2)

    load_own = pltpu.make_async_copy(rhs_hbm.at[0, 0], raw, load_sem.at[0])
    load_m = pltpu.make_async_copy(m_hbm.at[0, 0], m_v, load_sem.at[1])
    load_j = pltpu.make_async_copy(j_hbm.at[0, 0], j_v, load_sem.at[2])
    load_own.start()
    load_m.start()
    load_j.start()

    barrier = pltpu.get_barrier_semaphore()

    @pl.loop(1, n)
    def _(d):
        pl.semaphore_signal(barrier, inc=1, device_id=(s, peer(d)), device_id_type=MESH)

    @pl.when(has_up)
    def _():
        pl.semaphore_signal(barrier, inc=1, device_id=(s - 1, c), device_id_type=MESH)

    @pl.when(has_down)
    def _():
        pl.semaphore_signal(barrier, inc=1, device_id=(s + 1, c), device_id_type=MESH)

    zero_tile = jnp.zeros(tile, BF16)
    for h in halves:
        for r in range(3):
            for t in range(cap):
                ext[r][h][base + c * cap + t] = zero_tile
        run[h, zero_slot] = jnp.zeros(tile, F32)

    def clear(start):
        for h in halves:
            for r in range(3):
                for t in range(ovl):
                    ext[r][h][rows + start + t] = zero_tile
            for r in range(2):
                for t in range(ovl):
                    ret_slab[r, h, start + t] = zero_tile

    @pl.when(jnp.logical_not(has_up))
    def _():
        clear(0)

    @pl.when(jnp.logical_not(has_down))
    def _():
        clear(ovl)

    def slab_copy(src, dst, r, h, mine, theirs, to):
        return pltpu.make_async_remote_copy(
            src_ref=src, dst_ref=dst, send_sem=send_sem.at[r, h, mine], recv_sem=recv_sem.at[r, h, theirs],
            device_id=(to, c), device_id_type=MESH,
        )

    def lend_up(e, r, h):
        return slab_copy(ext[e][h].at[pl.ds(0, ovl)], ext[e][h].at[pl.ds(rows + ovl, ovl)], r, h, up_i, down_i, s - 1)

    def lend_down(e, r, h):
        return slab_copy(ext[e][h].at[pl.ds(rows - ovl, ovl)], ext[e][h].at[pl.ds(rows, ovl)], r, h, down_i, up_i, s + 1)

    def lend_cross(e, r, h, d):
        return pltpu.make_async_remote_copy(
            src_ref=send_buf.at[e, h, d - 1], dst_ref=ext[e][h].at[pl.ds(base + c * cap, cap)],
            send_sem=send_sem.at[r, h, d], recv_sem=recv_sem.at[r, h, n - d],
            device_id=(s, peer(d)), device_id_type=MESH,
        )

    def got_cross(e, r, h, d):
        return pltpu.make_async_remote_copy(
            src_ref=send_buf.at[e, h, d - 1], dst_ref=ext[e][h].at[pl.ds(base + peer(d) * cap, cap)],
            send_sem=send_sem.at[r, h, d], recv_sem=recv_sem.at[r, h, d],
            device_id=(s, peer(d)), device_id_type=MESH,
        )

    def got_up(e, r, h):
        return slab_copy(ext[e][h].at[pl.ds(0, ovl)], ext[e][h].at[pl.ds(rows, ovl)], r, h, up_i, up_i, s - 1)

    def got_down(e, r, h):
        return slab_copy(ext[e][h].at[pl.ds(0, ovl)], ext[e][h].at[pl.ds(rows + ovl, ovl)], r, h, down_i, down_i, s + 1)

    def lend_slab(e, r, h):
        @pl.when(has_up)
        def _():
            lend_up(e, r, h).start()

        @pl.when(has_down)
        def _():
            lend_down(e, r, h).start()

    def lend_rows(e, r, h):
        @pl.loop(0, n - 1)
        def _(step):
            d = order(step)
            q = peer(d)
            for t in range(cap):
                picked = own[e][h][targets[0, 0, t, q]]
                used = t < counts[0, 0, q]
                send_buf[e, h, d - 1, t] = jnp.where(used, picked, jnp.zeros_like(picked))
            lend_cross(e, r, h, d).start()

    def await_lent(e, r, h):
        @pl.when(has_up)
        def _():
            got_up(e, r, h).wait_recv()

        @pl.when(has_down)
        def _():
            got_down(e, r, h).wait_recv()

        @pl.loop(1, n)
        def _(d):
            got_cross(e, r, h, d).wait_recv()

    def finish_lend(e, r, h):
        @pl.when(has_up)
        def _():
            lend_up(e, r, h).wait_send()

        @pl.when(has_down)
        def _():
            lend_down(e, r, h).wait_send()

        @pl.loop(1, n)
        def _(d):
            lend_cross(e, r, h, d).wait_send()

    def back_up(a, r, h):
        return slab_copy(part.at[a, h, pl.ds(rows, ovl)], ret_slab.at[a, h, pl.ds(ovl, ovl)], r, h, up_i, down_i, s - 1)

    def back_down(a, r, h):
        return slab_copy(part.at[a, h, pl.ds(rows + ovl, ovl)], ret_slab.at[a, h, pl.ds(0, ovl)], r, h, down_i, up_i, s + 1)

    def home_up(a, r, h):
        return slab_copy(part.at[a, h, pl.ds(rows, ovl)], ret_slab.at[a, h, pl.ds(0, ovl)], r, h, up_i, up_i, s - 1)

    def home_down(a, r, h):
        return slab_copy(part.at[a, h, pl.ds(rows, ovl)], ret_slab.at[a, h, pl.ds(ovl, ovl)], r, h, down_i, down_i, s + 1)

    def back_cross(a, r, h, d):
        return pltpu.make_async_remote_copy(
            src_ref=part.at[a, h, pl.ds(base + peer(d) * cap, cap)], dst_ref=ret.at[a, h, n - d - 1],
            send_sem=send_sem.at[r, h, d], recv_sem=recv_sem.at[r, h, n - d],
            device_id=(s, peer(d)), device_id_type=MESH,
        )

    def home_cross(a, r, h, d):
        return pltpu.make_async_remote_copy(
            src_ref=part.at[a, h, pl.ds(base + peer(d) * cap, cap)], dst_ref=ret.at[a, h, d - 1],
            send_sem=send_sem.at[r, h, d], recv_sem=recv_sem.at[r, h, d],
            device_id=(s, peer(d)), device_id_type=MESH,
        )

    def row_product(blocks, cols, e, h, i, k0=0):
        left = jnp.concatenate([ext[e][h][cols[0, k, 0, i]] for k in range(k0, kcount)], axis=1)
        right = jnp.concatenate([blocks[i, k] for k in range(k0, kcount)], axis=1)
        return lax.dot_general(left, right, (((1,), (1,)), ((), ())), preferred_element_type=F32)

    def partial_row(a, e, h, i):
        part[a, h, i] = row_product(m_v, m_cols, e, h, i).astype(BF16)

    def apply_margins(a, e, r, h):
        @pl.loop(0, n - 1)
        def _(step):
            d = order(step)
            first_row = base + peer(d) * cap
            for t in range(cap):
                partial_row(a, e, h, first_row + t)
            back_cross(a, r, h, d).start()

        @pl.loop(0, 2 * ovl // 4)
        def _(g):
            for t in range(4):
                partial_row(a, e, h, rows + 4 * g + t)

        @pl.when(has_up)
        def _():
            back_up(a, r, h).start()

        @pl.when(has_down)
        def _():
            back_down(a, r, h).start()

    def apply_owned(a, e, h):
        @pl.loop(0, rows // 4)
        def _(g):
            for t in range(4):
                partial_row(a, e, h, 4 * g + t)

    def await_returns(a, r, h):
        @pl.loop(1, n)
        def _(d):
            home_cross(a, r, h, d).wait_recv()
            for t in range(cap):
                p = (d - 1) * cap + t
                run[h, p] = ret[a, h, d - 1, t].astype(F32) + run[h, prev[p]]

        @pl.when(has_up)
        def _():
            home_up(a, r, h).wait_recv()

        @pl.when(has_down)
        def _():
            home_down(a, r, h).wait_recv()

    def finish_return(a, r, h):
        @pl.when(has_up)
        def _():
            back_up(a, r, h).wait_send()

        @pl.when(has_down)
        def _():
            back_down(a, r, h).wait_send()

        @pl.loop(1, n)
        def _(d):
            back_cross(a, r, h, d).wait_send()

    def assembled(a, h, body):
        def total(i):
            return part[a, h, i].astype(F32) + run[h, last[i]]

        @pl.loop(0, ovl)
        def _(i):
            body(h, i, total(i) + ret_slab[a, h, i].astype(F32))

        @pl.loop(0, ovl)
        def _(t):
            i = rows - ovl + t
            body(h, i, total(i) + ret_slab[a, h, ovl + t].astype(F32))

        @pl.loop(ovl, rows - ovl)
        def _(i):
            body(h, i, total(i))

    load_own.wait()

    def turn(i):
        turned = raw[i].T
        for h in halves:
            ext[0][h][i] = turned[h * width : (h + 1) * width]

    @pl.loop(0, ovl)
    def _(i):
        turn(i)
        turn(rows - ovl + i)

    pl.semaphore_wait(barrier, n - 1 + has_up.astype(jnp.int32) + has_down.astype(jnp.int32))

    for h in halves:
        lend_slab(0, 0, h)

    @pl.loop(0, n - 1)
    def _(step):
        d = order(step)
        q = peer(d)
        for t in range(cap):
            picked = raw[targets[0, 0, t, q]]
            used = t < counts[0, 0, q]
            turned = jnp.where(used, picked, jnp.zeros_like(picked)).T
            for h in halves:
                send_buf[0, h, d - 1, t] = turned[h * width : (h + 1) * width]
        lend_cross(0, 0, 0, d).start()

    @pl.loop(0, n - 1)
    def _(step):
        lend_cross(0, 0, 1, order(step)).start()

    @pl.loop(ovl, rows - ovl)
    def _(i):
        turn(i)

    def key_of(p):
        q = peer(p // cap + 1)
        t = lax.rem(p, cap)
        return jnp.where(t < counts[0, 0, q], targets[0, 0, t, q], -1)

    @pl.loop(0, rows)
    def _(i):
        last[i] = zero_slot

    keys = [key_of(p) for p in range(slots)]
    for p in range(slots):
        found = zero_slot
        for p2 in range(p):
            found = jnp.where(keys[p2] == keys[p], p2, found)
        prev[p] = jnp.where(keys[p] < 0, zero_slot, found)

    @pl.loop(0, rows)
    def _(i):
        found = zero_slot
        for p in range(slots):
            found = jnp.where(keys[p] == i, p, found)
        last[i] = found

    load_m.wait()
    load_j.wait()

    def put_first(h, i, value):
        rounded = value.astype(BF16)
        own[1][h][i] = rounded
        ext[1][h][i] = rounded

    def put_second(h, i, value):
        second = (own[1][h][i].astype(F32) + value).astype(BF16)
        out_ref[0, 0, i, :, h * width : (h + 1) * width] = second.T

    def first_and_lend(h):
        await_returns(0, 1, h)
        assembled(0, h, put_first)
        lend_slab(1, 2, h)
        lend_rows(1, 2, h)

    def residual_and_lend(h):
        @pl.loop(0, rows // 4)
        def _(g):
            for t in range(4):
                i = 4 * g + t
                image = lax.dot_general(
                    own[1][h][i], j_v[i, 0], (((1,), (1,)), ((), ())), preferred_element_type=F32
                )
                acc[i] = ext[0][h][i].astype(F32) - image

        await_lent(1, 2, h)

        @pl.loop(0, rows // 4)
        def _(g):
            for t in range(4):
                i = 4 * g + t
                rounded = (acc[i] - row_product(j_v, j_cols, 1, h, i, 1)).astype(BF16)
                own[2][h][i] = rounded
                ext[2][h][i] = rounded

        lend_slab(2, 3, h)
        lend_rows(2, 3, h)

    def second_half(h):
        await_returns(1, 4, h)
        assembled(1, h, put_second)

    for a, e, r, finish in ((0, 0, 0, first_and_lend), (1, 2, 3, second_half)):
        await_lent(e, r, 0)
        apply_margins(a, e, r + 1, 0)
        apply_owned(a, e, 0)
        await_lent(e, r, 1)
        apply_margins(a, e, r + 1, 1)
        if a == 1:
            apply_owned(a, e, 1)
        finish(0)
        if a == 0:
            apply_owned(a, e, 1)
        finish(1)
        if a == 0:
            residual_and_lend(0)
            residual_and_lend(1)

    for h in halves:
        finish_lend(0, 0, h)
        finish_return(0, 1, h)
        finish_lend(1, 2, h)
        finish_lend(2, 3, h)
        finish_return(1, 4, h)


def solution(mesh):
    n_slab = mesh.shape["slab"]
    n = mesh.shape["cross"]

    def per_device(rhs, m_blocks, m_cols, j_blocks, j_cols, send_list, send_count):
        rows, blk, nv = rhs.shape[2:]
        total_rows, kcount = m_blocks.shape[2:4]
        cap = send_list.shape[3]
        ovl = (total_rows - rows - n * cap) // 2
        slots = (n - 1) * cap
        tile = (nv // 2, blk)
        smem = pl.BlockSpec(memory_space=pltpu.SMEM)
        hbm = pl.BlockSpec(memory_space=pl.ANY)
        return pl.pallas_call(
            functools.partial(kernel, n_slab, n, ovl),
            out_shape=jax.ShapeDtypeStruct(rhs.shape, rhs.dtype),
            in_specs=[hbm, hbm, hbm, smem, smem, smem, smem],
            out_specs=pl.BlockSpec(memory_space=pltpu.VMEM),
            scratch_shapes=[
                pltpu.VMEM(m_blocks.shape[2:], BF16),
                pltpu.VMEM(j_blocks.shape[2:], BF16),
                pltpu.VMEM((rows, blk, nv), BF16),
                *([pltpu.VMEM((rows,) + tile, BF16)] * 4),
                *([pltpu.VMEM((total_rows,) + tile, BF16)] * 6),
                pltpu.VMEM((2, 2, total_rows) + tile, BF16),
                pltpu.VMEM((3, 2, n - 1, cap) + tile, BF16),
                pltpu.VMEM((2, 2, n - 1, cap) + tile, BF16),
                pltpu.VMEM((2, 2, 2 * ovl) + tile, BF16),
                pltpu.VMEM((2, slots + 1) + tile, F32),
                pltpu.VMEM((rows,) + tile, F32),
                pltpu.SMEM((slots,), jnp.int32),
                pltpu.SMEM((rows,), jnp.int32),
                pltpu.SemaphoreType.DMA((3,)),
                pltpu.SemaphoreType.DMA((5, 2, n + 2)),
                pltpu.SemaphoreType.DMA((5, 2, n + 2)),
            ],
            compiler_params=pltpu.CompilerParams(
                collective_id=0, has_side_effects=True, vmem_limit_bytes=60 * 1024 * 1024
            ),
        )(
            rhs, m_blocks, j_blocks, m_cols.transpose(0, 3, 1, 2), j_cols.transpose(0, 3, 1, 2),
            send_list.transpose(0, 1, 3, 2), send_count,
        )

    return jax.shard_map(
        per_device,
        mesh=mesh,
        in_specs=(
            P("slab", "cross", None, None, None),
            P("slab", "cross", None, None, None, None),
            P("slab", "cross", None, None),
            P("slab", "cross", None, None, None, None),
            P("slab", "cross", None, None),
            P("slab", "cross", None, None),
            P("slab", "cross", None),
        ),
        out_specs=P("slab", "cross", None, None, None),
        check_vma=False,
    )
```

```python
import functools

import jax
import jax.numpy as jnp
from jax import lax
from jax.experimental import pallas as pl
from jax.experimental.pallas import tpu as pltpu
from jax.sharding import PartitionSpec as P

MESH = pl.DeviceIdType.MESH
F32 = jnp.float32
BF16 = jnp.bfloat16


def kernel(
    n_slab, n, ovl,
    rhs_hbm, m_hbm, j_hbm, m_cols, j_cols, targets, counts,
    out_ref,
    m_v, j_v, own0, own1, own2, ext0, ext1, ext2, part, send_buf, ret, ret_slab, run, acc,
    prev, last, load_sem, send_sem, recv_sem,
):
    s = lax.axis_index("slab")
    c = lax.axis_index("cross")
    own = (own0, own1, own2)
    ext = (ext0, ext1, ext2)
    rows = own0.shape[0]
    cap = send_buf.shape[2]
    kcount = m_v.shape[1]
    base = rows + 2 * ovl
    slots = (n - 1) * cap
    zero_slot = slots
    up_i, down_i = n, n + 1
    has_up = s > 0
    has_down = s < n_slab - 1

    def peer(d):
        return lax.rem(c + d, n)

    def order(t):
        return n // 2 + (1 - 2 * lax.rem(t, 2)) * ((t + 1) // 2)

    load_own = pltpu.make_async_copy(rhs_hbm.at[0, 0], own0, load_sem.at[0])
    load_ext = pltpu.make_async_copy(rhs_hbm.at[0, 0], ext0.at[pl.ds(0, rows)], load_sem.at[1])
    load_m = pltpu.make_async_copy(m_hbm.at[0, 0], m_v, load_sem.at[2])
    load_j = pltpu.make_async_copy(j_hbm.at[0, 0], j_v, load_sem.at[3])
    load_own.start()
    load_ext.start()
    load_m.start()
    load_j.start()

    barrier = pltpu.get_barrier_semaphore()

    @pl.loop(1, n)
    def _(d):
        pl.semaphore_signal(barrier, inc=1, device_id=(s, peer(d)), device_id_type=MESH)

    @pl.when(has_up)
    def _():
        pl.semaphore_signal(barrier, inc=1, device_id=(s - 1, c), device_id_type=MESH)

    @pl.when(has_down)
    def _():
        pl.semaphore_signal(barrier, inc=1, device_id=(s + 1, c), device_id_type=MESH)

    zero_tile = jnp.zeros(own0.shape[1:], BF16)
    for r in range(3):
        for t in range(cap):
            ext[r][base + c * cap + t] = zero_tile

    @pl.when(jnp.logical_not(has_up))
    def _():
        for r in range(3):
            for t in range(ovl):
                ext[r][rows + t] = zero_tile
        for r in range(2):
            for t in range(ovl):
                ret_slab[r, t] = zero_tile

    @pl.when(jnp.logical_not(has_down))
    def _():
        for r in range(3):
            for t in range(ovl):
                ext[r][rows + ovl + t] = zero_tile
        for r in range(2):
            for t in range(ovl):
                ret_slab[r, ovl + t] = zero_tile

    run[zero_slot] = jnp.zeros(own0.shape[1:], F32)

    def slab_copy(src, dst, r, mine, theirs, to):
        return pltpu.make_async_remote_copy(
            src_ref=src, dst_ref=dst, send_sem=send_sem.at[r, mine], recv_sem=recv_sem.at[r, theirs],
            device_id=(to, c), device_id_type=MESH,
        )

    def lend_up(e, r):
        return slab_copy(ext[e].at[pl.ds(0, ovl)], ext[e].at[pl.ds(rows + ovl, ovl)], r, up_i, down_i, s - 1)

    def lend_down(e, r):
        return slab_copy(ext[e].at[pl.ds(rows - ovl, ovl)], ext[e].at[pl.ds(rows, ovl)], r, down_i, up_i, s + 1)

    def lend_cross(e, r, d):
        return pltpu.make_async_remote_copy(
            src_ref=send_buf.at[e, d - 1], dst_ref=ext[e].at[pl.ds(base + c * cap, cap)],
            send_sem=send_sem.at[r, d], recv_sem=recv_sem.at[r, n - d],
            device_id=(s, peer(d)), device_id_type=MESH,
        )

    def got_cross(e, r, d):
        return pltpu.make_async_remote_copy(
            src_ref=send_buf.at[e, d - 1], dst_ref=ext[e].at[pl.ds(base + peer(d) * cap, cap)],
            send_sem=send_sem.at[r, d], recv_sem=recv_sem.at[r, d],
            device_id=(s, peer(d)), device_id_type=MESH,
        )

    def got_up(e, r):
        return slab_copy(ext[e].at[pl.ds(0, ovl)], ext[e].at[pl.ds(rows, ovl)], r, up_i, up_i, s - 1)

    def got_down(e, r):
        return slab_copy(ext[e].at[pl.ds(0, ovl)], ext[e].at[pl.ds(rows + ovl, ovl)], r, down_i, down_i, s + 1)

    def lend_slab(e, r):
        @pl.when(has_up)
        def _():
            lend_up(e, r).start()

        @pl.when(has_down)
        def _():
            lend_down(e, r).start()

    def lend_rows(e, r):
        @pl.loop(0, n - 1)
        def _(step):
            d = order(step)
            q = peer(d)
            for t in range(cap):
                picked = own[e][targets[0, 0, t, q]]
                used = t < counts[0, 0, q]
                send_buf[e, d - 1, t] = jnp.where(used, picked, jnp.zeros_like(picked))
            lend_cross(e, r, d).start()

    def await_lent(e, r):
        @pl.when(has_up)
        def _():
            got_up(e, r).wait_recv()

        @pl.when(has_down)
        def _():
            got_down(e, r).wait_recv()

        @pl.loop(1, n)
        def _(d):
            got_cross(e, r, d).wait_recv()

    def finish_lend(e, r):
        @pl.when(has_up)
        def _():
            lend_up(e, r).wait_send()

        @pl.when(has_down)
        def _():
            lend_down(e, r).wait_send()

        @pl.loop(1, n)
        def _(d):
            lend_cross(e, r, d).wait_send()

    def back_up(a, r):
        return slab_copy(part.at[a, pl.ds(rows, ovl)], ret_slab.at[a, pl.ds(ovl, ovl)], r, up_i, down_i, s - 1)

    def back_down(a, r):
        return slab_copy(part.at[a, pl.ds(rows + ovl, ovl)], ret_slab.at[a, pl.ds(0, ovl)], r, down_i, up_i, s + 1)

    def home_up(a, r):
        return slab_copy(part.at[a, pl.ds(rows, ovl)], ret_slab.at[a, pl.ds(0, ovl)], r, up_i, up_i, s - 1)

    def home_down(a, r):
        return slab_copy(part.at[a, pl.ds(rows, ovl)], ret_slab.at[a, pl.ds(ovl, ovl)], r, down_i, down_i, s + 1)

    def back_cross(a, r, d):
        return pltpu.make_async_remote_copy(
            src_ref=part.at[a, pl.ds(base + peer(d) * cap, cap)], dst_ref=ret.at[a, n - d - 1],
            send_sem=send_sem.at[r, d], recv_sem=recv_sem.at[r, n - d],
            device_id=(s, peer(d)), device_id_type=MESH,
        )

    def home_cross(a, r, d):
        return pltpu.make_async_remote_copy(
            src_ref=part.at[a, pl.ds(base + peer(d) * cap, cap)], dst_ref=ret.at[a, d - 1],
            send_sem=send_sem.at[r, d], recv_sem=recv_sem.at[r, d],
            device_id=(s, peer(d)), device_id_type=MESH,
        )

    def row_product(blocks, cols, e, i, k0=0):
        left = jnp.concatenate([blocks[i, k] for k in range(k0, kcount)], axis=1)
        right = jnp.concatenate([ext[e][cols[0, k, 0, i]] for k in range(k0, kcount)], axis=0)
        return jnp.dot(left, right, preferred_element_type=F32)

    def partial_row(a, e, i):
        part[a, i] = row_product(m_v, m_cols, e, i).astype(BF16)

    def apply_and_return(a, e, r):
        @pl.loop(0, n - 1)
        def _(step):
            d = order(step)
            first_row = base + peer(d) * cap
            for t in range(cap):
                partial_row(a, e, first_row + t)
            back_cross(a, r, d).start()

        @pl.loop(0, 2 * ovl // 4)
        def _(g):
            for t in range(4):
                partial_row(a, e, rows + 4 * g + t)

        @pl.when(has_up)
        def _():
            back_up(a, r).start()

        @pl.when(has_down)
        def _():
            back_down(a, r).start()

        @pl.loop(0, rows // 4)
        def _(g):
            for t in range(4):
                partial_row(a, e, 4 * g + t)

    def await_returns(a, r):
        @pl.loop(1, n)
        def _(d):
            home_cross(a, r, d).wait_recv()
            for t in range(cap):
                p = (d - 1) * cap + t
                run[p] = ret[a, d - 1, t].astype(F32) + run[prev[p]]

        @pl.when(has_up)
        def _():
            home_up(a, r).wait_recv()

        @pl.when(has_down)
        def _():
            home_down(a, r).wait_recv()

    def finish_return(a, r):
        @pl.when(has_up)
        def _():
            back_up(a, r).wait_send()

        @pl.when(has_down)
        def _():
            back_down(a, r).wait_send()

        @pl.loop(1, n)
        def _(d):
            back_cross(a, r, d).wait_send()

    def assembled(a, body):
        def total(i):
            return part[a, i].astype(F32) + run[last[i]]

        @pl.loop(0, ovl)
        def _(t):
            i = rows - ovl + t
            body(t, total(t) + ret_slab[a, t].astype(F32))
            body(i, total(i) + ret_slab[a, ovl + t].astype(F32))

        @pl.loop(0, (rows - 2 * ovl) // 4)
        def _(g):
            for t in range(4):
                i = ovl + 4 * g + t
                body(i, total(i))

    load_own.wait()
    load_ext.wait()

    pl.semaphore_wait(barrier, n - 1 + has_up.astype(jnp.int32) + has_down.astype(jnp.int32))

    lend_slab(0, 0)
    lend_rows(0, 0)

    def key_of(p):
        q = peer(p // cap + 1)
        t = lax.rem(p, cap)
        return jnp.where(t < counts[0, 0, q], targets[0, 0, t, q], -1)

    @pl.loop(0, rows)
    def _(i):
        last[i] = zero_slot

    keys = [key_of(p) for p in range(slots)]
    for p in range(slots):
        found = zero_slot
        for p2 in range(p):
            found = jnp.where(keys[p2] == keys[p], p2, found)
        prev[p] = jnp.where(keys[p] < 0, zero_slot, found)

    @pl.loop(0, rows)
    def _(i):
        found = zero_slot
        for p in range(slots):
            found = jnp.where(keys[p] == i, p, found)
        last[i] = found

    load_m.wait()
    load_j.wait()
    await_lent(0, 0)

    apply_and_return(0, 0, 1)
    await_returns(0, 1)

    def put_first(i, value):
        rounded = value.astype(BF16)
        own[1][i] = rounded
        ext[1][i] = rounded

    assembled(0, put_first)

    lend_slab(1, 2)
    lend_rows(1, 2)

    @pl.loop(0, rows // 4)
    def _(g):
        for t in range(4):
            i = 4 * g + t
            acc[i] = own[0][i].astype(F32) - jnp.dot(j_v[i, 0], own[1][i], preferred_element_type=F32)

    await_lent(1, 2)

    @pl.loop(0, rows // 4)
    def _(g):
        for t in range(4):
            i = 4 * g + t
            rounded = (acc[i] - row_product(j_v, j_cols, 1, i, 1)).astype(BF16)
            own[2][i] = rounded
            ext[2][i] = rounded

    lend_slab(2, 3)
    lend_rows(2, 3)
    await_lent(2, 3)

    apply_and_return(1, 2, 4)
    await_returns(1, 4)

    def put_second(i, value):
        out_ref[0, 0, i] = (own[1][i].astype(F32) + value).astype(BF16)

    assembled(1, put_second)

    finish_lend(0, 0)
    finish_return(0, 1)
    finish_lend(1, 2)
    finish_lend(2, 3)
    finish_return(1, 4)


def solution(mesh):
    n_slab = mesh.shape["slab"]
    n = mesh.shape["cross"]

    def per_device(rhs, m_blocks, m_cols, j_blocks, j_cols, send_list, send_count):
        rows, blk, nv = rhs.shape[2:]
        total_rows, kcount = m_blocks.shape[2:4]
        cap = send_list.shape[3]
        ovl = (total_rows - rows - n * cap) // 2
        slots = (n - 1) * cap
        tile = (blk, nv)
        smem = pl.BlockSpec(memory_space=pltpu.SMEM)
        hbm = pl.BlockSpec(memory_space=pltpu.HBM)
        return pl.pallas_call(
            functools.partial(kernel, n_slab, n, ovl),
            out_shape=pltpu.VMEM(rhs.shape, rhs.dtype),
            in_specs=[hbm, hbm, hbm, smem, smem, smem, smem],
            out_specs=pl.BlockSpec(memory_space=pltpu.VMEM),
            scratch_shapes=[
                pltpu.VMEM(m_blocks.shape[2:], BF16),
                pltpu.VMEM(j_blocks.shape[2:], BF16),
                *([pltpu.VMEM((rows,) + tile, BF16)] * 3),
                *([pltpu.VMEM((total_rows,) + tile, BF16)] * 3),
                pltpu.VMEM((2, total_rows) + tile, BF16),
                pltpu.VMEM((3, n - 1, cap) + tile, BF16),
                pltpu.VMEM((2, n - 1, cap) + tile, BF16),
                pltpu.VMEM((2, 2 * ovl) + tile, BF16),
                pltpu.VMEM((slots + 1,) + tile, F32),
                pltpu.VMEM((rows,) + tile, F32),
                pltpu.SMEM((slots,), jnp.int32),
                pltpu.SMEM((rows,), jnp.int32),
                pltpu.SemaphoreType.DMA((4,)),
                pltpu.SemaphoreType.DMA((5, n + 2)),
                pltpu.SemaphoreType.DMA((5, n + 2)),
            ],
            compiler_params=pltpu.CompilerParams(
                collective_id=0, has_side_effects=True, vmem_limit_bytes=60 * 1024 * 1024
            ),
        )(
            rhs, m_blocks, j_blocks, m_cols.transpose(0, 3, 1, 2), j_cols.transpose(0, 3, 1, 2),
            send_list.transpose(0, 1, 3, 2), send_count,
        )

    return jax.shard_map(
        per_device,
        mesh=mesh,
        in_specs=(
            P("slab", "cross", None, None, None),
            P("slab", "cross", None, None, None, None),
            P("slab", "cross", None, None),
            P("slab", "cross", None, None, None, None),
            P("slab", "cross", None, None),
            P("slab", "cross", None, None),
            P("slab", "cross", None),
        ),
        out_specs=P("slab", "cross", None, None, None),
        check_vma=False,
    )
```
